32 devices in a mesh: groups: 2 (over x), layer: 4 (over z), iface: 4 (over y, core).
Axes of the slice: x: 2, y: 2, z: 4, core: 2. Of those that a mesh axis runs over, the one named last changes fastest.
Arguments:
- top_trace: bfloat16 [6, 2, 8192, 128], P('groups', None, 'iface'), parts along dimension 0, may hold values from -6 to 6
- sources: bfloat16 [4, 8, 2, 8192, 128], P('layer', 'groups', None, 'iface'), parts along dimension 1, may hold values from -6 to 6
- near_blocks: bfloat16 [4, 2, 32, 8, 256, 256], P('layer', None, 'iface'), may hold values from -0.0625 to 0.0625
- near_index: int32 [32, 8], P('iface'), may hold values from 0 to 31, as said below
- far_left: bfloat16 [4, 2, 64, 8192], P('layer', None, None, 'iface'), may hold values from -0.25 to 0.25
- far_right: bfloat16 [4, 2, 64, 8192], P('layer', None, None, 'iface'), may hold values from -0.046875 to 0.046875
- assign: int32 [4, 3], replicated, may hold values from 0 to 3
Outputs:
- traces: bfloat16 [4, 6, 2, 8192, 128], P('layer', 'groups', None, 'iface'), parts along dimension 1
The draws below stay inside these ranges and needn't reach their ends.
There are 2 independent parts, one for each index of `groups`. The reference program is written for one: setup_inputs(seed, part) draws one part's arguments, and reference() takes and returns one part's arrays. A program takes and returns all parts, laid end to end along the dimension named above; an argument that names none is the same for every part. Nothing has to cross between parts.
Inputs may be any that keep to these rules, and one draw needn't show every extreme that they name: near_index[b, k] = clip(b + o, 0, 8192 / 256 - 1) with the offsets o of a row distinct in -4 .. 4.
All inputs are finite; a program needn't handle non-finite values.
Results may differ from the reference program's by a relative error of at most 0.012.
Values may be sent and summed in bfloat16 or wider, within the bound.
A program may use at most 128 MiB of HBM per device.

```python
import jax
import jax.numpy as jnp

NI = 8192
BLK = 256
NEAR = 8
BAND = 4
RANK = 64
P_SIZE = 128
PANELS = 3
BANK = 4
LAYERS = 4


def draw_near_index(key, part):
    count = NI // BLK
    width = 2 * BAND + 1
    scores = jax.random.randint(key, (count, width), 0, 1 << 20) * width + jnp.arange(width)[None, :]
    order = jnp.argsort(scores, axis=1, stable=True)
    offsets = order[:, :NEAR] - BAND
    return jnp.clip(jnp.arange(count)[:, None] + offsets, 0, count - 1).astype(jnp.int32)


def touch_ends(array, own_key, low, high):
    place = [jax.random.randint(jax.random.fold_in(own_key, axis), (), 0, length) for axis, length in enumerate(array.shape)]
    main_axis = array.shape.index(max(array.shape))
    neighbour = place[:main_axis] + [(place[main_axis] + 1) % array.shape[main_axis]] + place[main_axis + 1:]
    return array.at[tuple(place)].set(low).at[tuple(neighbour)].set(high)


def block_scale(key, extent, pieces, least, largest):
    gain = 1.0
    for position, parts in pieces:
        draws = jax.random.uniform(jax.random.fold_in(jax.random.fold_in(key, 6), position), (parts,), jnp.float32, least / len(pieces), largest / len(pieces))
        gain = gain * jnp.repeat(jnp.exp(draws), extent[position] // parts).reshape((-1,) + (1,) * (len(extent) - 1 - position))
    return gain


def normal_values(rng, shape, deviation, bound, pieces=(), held_as=jnp.bfloat16):
    drawn = deviation * jax.random.normal(rng, shape, jnp.float32)
    if pieces:
        drawn = drawn * block_scale(rng, shape, pieces, -0.22, 0.18)
    return jnp.clip(drawn, -bound, bound).astype(held_as)


def setup_inputs(seed: int = 0, part: int = 0) -> dict:
    seeds = jax.random.split(jax.random.key(seed), 8)
    own_keys = jax.random.split(jax.random.fold_in(seeds[7], part), 8)
    return {
        "top_trace": normal_values(own_keys[0], (PANELS, 2, NI, P_SIZE), 1.0, 6.0, ((2, 4),)),
        "sources": normal_values(own_keys[1], (LAYERS, BANK, 2, NI, P_SIZE), 1.0, 6.0, ((0, 4), (3, 4))),
        "near_blocks": normal_values(seeds[2], (LAYERS, 2, NI // BLK, NEAR, BLK, BLK), (4 * NEAR * BLK) ** -0.5, 0.0625, ((0, 4), (2, 4))),
        "near_index": draw_near_index(jax.random.fold_in(seeds[7], 71), part),
        "far_left": normal_values(seeds[4], (LAYERS, 2, RANK, NI), (8 * RANK) ** -0.5, 0.25, ((0, 4), (3, 4))),
        "far_right": normal_values(seeds[5], (LAYERS, 2, RANK, NI), (2 * NI) ** -0.5, 0.046875, ((0, 4), (3, 4))),
        "assign": touch_ends(jax.random.randint(seeds[6], (LAYERS, PANELS), 0, BANK), jax.random.fold_in(seeds[6], 1), 0, BANK - 1).astype(jnp.int32),
    }


def near_apply(trace_in, blocks_mat, near_index):
    count = NI // BLK
    shaped = trace_in.reshape(2, count, BLK, P_SIZE).astype(jnp.float32)
    picked = shaped[:, near_index]
    mats = blocks_mat.astype(jnp.float32)
    part_real = jnp.einsum("jkab,cjkbp->cjap", mats[0], picked)
    part_imag = jnp.einsum("jkab,cjkbp->cjap", mats[1], picked)
    result = jnp.stack([part_real[0] - part_imag[1], part_real[1] + part_imag[0]])
    return result.reshape(2, NI, P_SIZE)


def far_apply(trace_in, left_mat, right_mat):
    def mult(mat, vec):
        return jnp.dot(mat, vec, preferred_element_type=jnp.float32)

    partial_value = jnp.stack([mult(right_mat[0], trace_in[0]) - mult(right_mat[1], trace_in[1]),
                         mult(right_mat[0], trace_in[1]) + mult(right_mat[1], trace_in[0])])
    coefficient = partial_value.astype(jnp.bfloat16)

    def lift(mat, vec):
        return jnp.einsum("ri,rp->ip", mat.astype(jnp.float32), vec.astype(jnp.float32))

    return jnp.stack([lift(left_mat[0], coefficient[0]) - lift(left_mat[1], coefficient[1]),
                      lift(left_mat[0], coefficient[1]) + lift(left_mat[1], coefficient[0])])


def reference(top_trace, sources, near_blocks, near_index, far_left, far_right, assign):
    per_layer = []
    for layer_pos in range(LAYERS):
        per_layer.append([])
    for panel_idx in range(PANELS):
        current = top_trace[panel_idx]
        for layer_pos in range(LAYERS):
            near_term = near_apply(current, near_blocks[layer_pos], near_index)
            far_term = far_apply(current, far_left[layer_pos], far_right[layer_pos])
            source_term = sources[layer_pos, assign[layer_pos, panel_idx]].astype(jnp.float32)
            current = (near_term + far_term + source_term).astype(jnp.bfloat16)
            per_layer[layer_pos].append(current)
    return jnp.stack([jnp.stack(items) for items in per_layer])
```

```python
import functools

import jax
import jax.numpy as jnp
from jax import lax
from jax.experimental import pallas as pl
from jax.experimental.pallas import tpu as pltpu
from jax.sharding import PartitionSpec as P

BLK = 256
BAND = 4
MESH = pl.DeviceIdType.MESH


def times_i(value):
    half = value.shape[1] // 2
    rolled = pltpu.roll(value, half, 1)
    lane = lax.broadcasted_iota(jnp.int32, value.shape, 1)
    return jnp.where(lane < half, -rolled, rolled)


def halo_list(blocks_dev):
    reach = -(-BAND // blocks_dev)
    pairs = []
    for j in range(blocks_dev):
        for d in range(1, reach + 1):
            if j >= d * blocks_dev - BAND:
                pairs.append((j, d, j - d * blocks_dev + BAND))
            if j < blocks_dev - d * blocks_dev + BAND:
                pairs.append((j, -d, j + d * blocks_dev + BAND))
    return pairs


def kernel(
    n_iface, n_layer, chunks, blocks_dev, near_count, rank,
    index_ref, top_ref, source_ref, near_hbm, left_ref, right_ref,
    out_ref,
    win, work, near, ucat, coef, ccat,
    z_send, z_recv, h_send, h_recv, f_send, f_recv, top_sem, near_sem,
):
    me = lax.axis_index("iface")
    layer = lax.axis_index("layer")
    halos = halo_list(blocks_dev)
    reach = -(-BAND // blocks_dev)
    has_up = layer > 0
    has_down = layer < n_layer - 1

    def top_copy(t):
        return pltpu.make_async_copy(
            top_ref.at[t], win.at[t, pl.ds(BAND, blocks_dev)], top_sem.at[t]
        )

    def near_copy(j, k):
        return pltpu.make_async_copy(
            near_hbm.at[:, j, k], near.at[:, j, :, pl.ds(k * BLK, BLK)], near_sem.at[j, k]
        )

    def z_copy(t, j):
        return pltpu.make_async_remote_copy(
            src_ref=out_ref.at[t, j],
            dst_ref=win.at[t, BAND + j],
            send_sem=z_send.at[t, j],
            recv_sem=z_recv.at[t, j],
            device_id={"layer": layer + 1},
            device_id_type=MESH,
        )

    def h_copy(t, q):
        j, d, place = halos[q]
        return pltpu.make_async_remote_copy(
            src_ref=win.at[t, BAND + j],
            dst_ref=win.at[t, place],
            send_sem=h_send.at[t, q],
            recv_sem=h_recv.at[t, q],
            device_id={"iface": me + d},
            device_id_type=MESH,
        )

    def inside(pos):
        return jnp.logical_and(pos >= 0, pos < n_iface)

    def f_copy(t, d):
        return pltpu.make_async_remote_copy(
            src_ref=coef.at[t, 0],
            dst_ref=coef.at[t, d],
            send_sem=f_send.at[t, d],
            recv_sem=f_recv.at[t, d],
            device_id={"iface": lax.rem(me + d, n_iface)},
            device_id_type=MESH,
        )

    @pl.when(layer == 0)
    def _():
        for t in range(chunks):
            top_copy(t).start()

    for j in range(blocks_dev):
        for k in range(near_count):
            near_copy(j, k).start()

    barrier = pltpu.get_barrier_semaphore()
    for d in range(1, n_iface):
        pl.semaphore_signal(
            barrier, inc=1, device_id={"iface": lax.rem(me + d, n_iface)}, device_id_type=MESH
        )

    @pl.when(has_up)
    def _():
        pl.semaphore_signal(
            barrier, inc=1, device_id={"layer": layer - 1}, device_id_type=MESH
        )

    @pl.when(has_down)
    def _():
        pl.semaphore_signal(
            barrier, inc=1, device_id={"layer": layer + 1}, device_id_type=MESH
        )

    neighbours = jnp.where(has_up, 1, 0) + jnp.where(has_down, 1, 0)
    pl.semaphore_wait(barrier, n_iface - 1 + neighbours)

    def chunk_step(t, carry):
        @pl.when(layer == 0)
        def _():
            top_copy(t).wait()

        partial = None
        for j in range(blocks_dev):
            @pl.when(has_up)
            def _():
                z_copy(t, j).wait_recv()

            for q, (hj, d, _place) in enumerate(halos):
                if hj == j:
                    @pl.when(inside(me + d))
                    def _():
                        h_copy(t, q).start()

            term = jnp.dot(
                right_ref[:, j * BLK : (j + 1) * BLK],
                win[t, BAND + j],
                preferred_element_type=jnp.float32,
            )
            partial = term if partial is None else partial + term
        coef[t, 0] = partial[:rank] + times_i(partial[rank:])
        for d in range(1, n_iface):
            f_copy(t, d).start()

        for q, (_j, d, _place) in enumerate(halos):
            @pl.when(inside(me - d))
            def _():
                h_copy(t, q).wait_recv()

        work[...] = win[t]
        for d in range(1, n_iface):
            f_copy(t, d).wait_recv()
        total = coef[t, 0]
        for d in range(1, n_iface):
            total = total + coef[t, d]
        total = total.astype(jnp.bfloat16)
        ccat[0:rank] = total
        ccat[rank : 2 * rank] = times_i(total.astype(jnp.float32)).astype(jnp.bfloat16)

        def row_step(j, inner):
            @pl.when(t == 0)
            def _():
                for k in range(near_count):
                    near_copy(j, k).wait()

            for k in range(near_count):
                ucat[k * BLK : (k + 1) * BLK] = work[index_ref[j, k]]
            pieces = []
            for c in range(2):
                pieces.append(
                    jnp.dot(near[c, j], ucat[...], preferred_element_type=jnp.float32)
                )
            far = jnp.dot(left_ref[j], ccat[...], preferred_element_type=jnp.float32)
            result = pieces[0] + times_i(pieces[1]) + far + source_ref[t, j].astype(jnp.float32)
            out_ref[t, j] = result.astype(jnp.bfloat16)

            @pl.when(has_down)
            def _():
                z_copy(t, j).start()

            return inner

        return lax.fori_loop(0, blocks_dev, row_step, carry)

    lax.fori_loop(0, chunks, chunk_step, 0)

    def drain(t, carry):
        for q, (_j, d, _place) in enumerate(halos):
            @pl.when(inside(me + d))
            def _():
                h_copy(t, q).wait_send()

        for d in range(1, n_iface):
            f_copy(t, d).wait_send()

        @pl.when(has_down)
        def _():
            for j in range(blocks_dev):
                z_copy(t, j).wait_send()

        return carry

    lax.fori_loop(0, chunks, drain, 0)


def packed(array):
    panels, _, rows, columns = array.shape
    half = columns // 2
    parts = [
        jnp.concatenate(
            [array[:, 0, :, h * half : (h + 1) * half], array[:, 1, :, h * half : (h + 1) * half]],
            axis=-1,
        )
        for h in range(2)
    ]
    return jnp.stack(parts, axis=1).reshape(panels * 2, rows // BLK, BLK, columns)


def unpacked(array, panels):
    _, blocks, _, columns = array.shape
    half = columns // 2
    array = array.reshape(panels, 2, blocks * BLK, columns)
    parts = [
        jnp.concatenate(
            [array[:, 0, :, c * half : (c + 1) * half], array[:, 1, :, c * half : (c + 1) * half]],
            axis=-1,
        )
        for c in range(2)
    ]
    return jnp.stack(parts, axis=1)


def per_device(n_iface, n_layer, top_trace, sources, near_blocks, near_index, far_left, far_right, assign):
    panels, _, rows_dev, columns = top_trace.shape
    blocks_dev = rows_dev // BLK
    near_count = near_index.shape[1]
    rank = far_left.shape[2]
    chunks = panels * 2
    layer_pos = lax.axis_index("layer")
    local_index = near_index - (lax.axis_index("iface") * blocks_dev - BAND)
    chosen = jnp.take(sources[0], assign[layer_pos], axis=0)
    top = packed(top_trace)
    source = packed(chosen)
    left = far_left[0].reshape(2 * rank, rows_dev).T.reshape(blocks_dev, BLK, 2 * rank)
    right = far_right[0].reshape(2 * rank, rows_dev)
    halo_count = len(halo_list(blocks_dev))
    window = blocks_dev + 2 * BAND
    vmem = pl.BlockSpec(memory_space=pltpu.VMEM)
    anywhere = pl.BlockSpec(memory_space=pl.ANY)
    dma = pltpu.SemaphoreType.DMA
    bf16 = jnp.bfloat16
    out = pl.pallas_call(
        functools.partial(kernel, n_iface, n_layer, chunks, blocks_dev, near_count, rank),
        out_shape=jax.ShapeDtypeStruct((chunks, blocks_dev, BLK, columns), bf16),
        in_specs=[
            pl.BlockSpec(memory_space=pltpu.SMEM), anywhere, vmem, anywhere, vmem, vmem,
        ],
        out_specs=vmem,
        scratch_shapes=[
            pltpu.VMEM((chunks, window, BLK, columns), bf16),
            pltpu.VMEM((window, BLK, columns), bf16),
            pltpu.VMEM((2, blocks_dev, BLK, near_count * BLK), bf16),
            pltpu.VMEM((near_count * BLK, columns), bf16),
            pltpu.VMEM((chunks, n_iface, rank, columns), jnp.float32),
            pltpu.VMEM((2 * rank, columns), bf16),
            dma((chunks, blocks_dev)),
            dma((chunks, blocks_dev)),
            dma((chunks, halo_count)),
            dma((chunks, halo_count)),
            dma((chunks, n_iface)),
            dma((chunks, n_iface)),
            dma((chunks,)),
            dma((blocks_dev, near_count)),
        ],
        compiler_params=pltpu.CompilerParams(collective_id=0, has_side_effects=True),
    )(local_index, top, source, near_blocks[0], left, right)
    return unpacked(out, panels)[None]


def solution(mesh):
    return jax.shard_map(
        functools.partial(per_device, mesh.shape["iface"], mesh.shape["layer"]),
        mesh=mesh,
        in_specs=(
            P("groups", None, "iface", None),
            P("layer", "groups", None, "iface", None),
            P("layer", None, "iface", None, None, None),
            P("iface", None),
            P("layer", None, None, "iface"),
            P("layer", None, None, "iface"),
            P(),
        ),
        out_specs=P("layer", "groups", None, "iface", None),
        check_vma=False,
    )
```
